128 devices in a mesh: seg: 8 (over x, core), tr: 16 (over z, y).
Axes of the slice: x: 4, y: 4, z: 4, core: 2. Of those that a mesh axis runs over, the one named last changes fastest.
Arguments:
- energies: float32 [1], replicated, may hold values from -0.1 to 0.1
- hamiltonian: bfloat16 [16, 768, 768], P('seg'), may hold values from -4 to 4
- coupling: bfloat16 [16, 768, 768], P('seg'), may hold values from -1.5 to 1.5
- seed_inverse: bfloat16 [2, 1, 16, 768, 768], P(None, None, 'seg'), may hold values from -2 to 2
- lead_green: bfloat16 [2, 1, 768, 768], P(None, None, None, 'tr'), may hold values from -1 to 1
Outputs:
- green: bfloat16 [2, 1, 16, 768, 768], P(None, None, 'seg', None, 'tr')
The draws below stay inside these ranges and needn't reach their ends.
All inputs are finite; a program needn't handle non-finite values.
Results may differ from the reference program's by a relative error of at most 0.025.
Values may be sent and summed in bfloat16 or wider, within the bound.
No kernel may reach another device: no remote copies, remote signals or barrier semaphores. Data moves between devices by JAX's collectives and lax.ppermute only.
A program may use at most 64 MiB of HBM per device.

```python
import jax
import jax.numpy as jnp

B = 768
ENERGIES = 1
SLABS = 16


broadening = 0.6


def level_values(key):
    return jax.random.uniform(jax.random.fold_in(key, 101), (SLABS, B), jnp.float32, -1.4, 1.4)


def hopping_values(key):
    raw = jax.random.normal(jax.random.fold_in(key, 102), (SLABS, B, B), jnp.float32)
    symmetric = (raw + jnp.swapaxes(raw, 1, 2)) * (0.25 / jnp.sqrt(2.0 * B))
    return symmetric * (1.0 - jnp.eye(B, dtype=jnp.float32))[None]


def energy_values(key):
    return jax.random.uniform(jax.random.fold_in(key, 103), (ENERGIES,), jnp.float32, -0.1, 0.1)


def draw_energies(key, part):
    return energy_values(key)


def draw_hamiltonian(key, part):
    levels = level_values(key)
    identity = jnp.eye(B, dtype=jnp.float32)
    return (hopping_values(key) + identity[None] * levels[:, :, None]).astype(jnp.bfloat16)


def draw_coupling(key, part):
    levels = level_values(key)
    strength = jnp.sqrt(0.8 * (levels * levels + broadening * broadening))
    raw = jnp.clip(jax.random.normal(jax.random.fold_in(key, 105), (SLABS, B, B), jnp.float32), -3.5, 3.5)
    noise = raw * (0.22 / jnp.sqrt(1.0 * B))
    identity = jnp.eye(B, dtype=jnp.float32)
    return (noise + identity[None] * strength[:, :, None]).astype(jnp.bfloat16)


def draw_seed_inverse(key, part):
    levels = level_values(key)
    hopping = hopping_values(key)
    energy = energy_values(key)
    offset = energy[:, None, None] - levels[None]
    denom = offset * offset + broadening * broadening
    inv_real = offset / denom
    inv_imag = -broadening / denom
    outer_real = inv_real[:, :, :, None] * inv_real[:, :, None, :] - inv_imag[:, :, :, None] * inv_imag[:, :, None, :]
    outer_imag = inv_real[:, :, :, None] * inv_imag[:, :, None, :] + inv_imag[:, :, :, None] * inv_real[:, :, None, :]
    identity = jnp.eye(B, dtype=jnp.float32)
    seed_real = identity * inv_real[:, :, :, None] - hopping[None] * outer_real
    seed_imag = identity * inv_imag[:, :, :, None] - hopping[None] * outer_imag
    return jnp.stack([seed_real, seed_imag]).astype(jnp.bfloat16)


def draw_lead_green(key, part):
    identity = jnp.eye(B, dtype=jnp.float32)
    diag_real = jax.random.uniform(jax.random.fold_in(key, 106), (ENERGIES, B), jnp.float32, -0.4, 0.4)
    diag_imag = jax.random.uniform(jax.random.fold_in(key, 107), (ENERGIES, B), jnp.float32, -0.8, -0.2)
    noise = jax.random.normal(jax.random.fold_in(key, 108), (2, ENERGIES, B, B), jnp.float32) * (0.3 / jnp.sqrt(1.0 * B))
    diagonal = jnp.stack([diag_real, diag_imag])[:, :, :, None] * identity
    return (noise + diagonal).astype(jnp.bfloat16)


def setup_inputs(seed: int = 0) -> dict:
    arg_keys = jax.random.split(jax.random.key(seed), 6)
    energies = draw_energies(jax.random.fold_in(arg_keys[5], 71), 0)
    hamiltonian = draw_hamiltonian(jax.random.fold_in(arg_keys[5], 71), 0)
    coupling = draw_coupling(jax.random.fold_in(arg_keys[5], 71), 0)
    seed_inverse = draw_seed_inverse(jax.random.fold_in(arg_keys[5], 71), 0)
    lead_green = draw_lead_green(jax.random.fold_in(arg_keys[5], 71), 0)
    return dict(energies=energies, hamiltonian=hamiltonian, coupling=coupling, seed_inverse=seed_inverse, lead_green=lead_green)


broadening = 0.6


def product(left, right):
    return jnp.dot(left, right, preferred_element_type=jnp.float32)


def pair_product(left_real, left_imag, right_real, right_imag):
    real_part = product(left_real, right_real) - product(left_imag, right_imag)
    imag_part = product(left_real, right_imag) + product(left_imag, right_real)
    return real_part, imag_part


def slab_step(energy, onsite, couple, seed_real, seed_imag, before_real, before_imag):
    weight_real = product(couple.T, seed_real).astype(jnp.bfloat16)
    weight_imag = product(couple.T, seed_imag).astype(jnp.bfloat16)
    summed_real, summed_imag = pair_product(before_real, before_imag, weight_real, weight_imag)
    carry_real = summed_real.astype(jnp.bfloat16)
    carry_imag = summed_imag.astype(jnp.bfloat16)
    seed_real32 = seed_real.astype(jnp.float32)
    seed_imag32 = seed_imag.astype(jnp.float32)
    probe_real = energy * seed_real32 - broadening * seed_imag32 - product(onsite, seed_real) - product(couple, carry_real)
    probe_imag = energy * seed_imag32 + broadening * seed_real32 - product(onsite, seed_imag) - product(couple, carry_imag)
    probe_real = probe_real.astype(jnp.bfloat16)
    probe_imag = probe_imag.astype(jnp.bfloat16)
    back_real, back_imag = pair_product(seed_real, seed_imag, probe_real, probe_imag)
    green_real = (2.0 * seed_real32 - back_real).astype(jnp.bfloat16)
    green_imag = (2.0 * seed_imag32 - back_imag).astype(jnp.bfloat16)
    return green_real, green_imag


def reference(energies, hamiltonian, coupling, seed_inverse, lead_green):
    results = []
    for energy_index in range(ENERGIES):
        before_real = lead_green[0, energy_index]
        before_imag = lead_green[1, energy_index]
        chain_blocks = []
        for slab_index in range(SLABS):
            before_real, before_imag = slab_step(energies[energy_index], hamiltonian[slab_index], coupling[slab_index], seed_inverse[0, energy_index, slab_index], seed_inverse[1, energy_index, slab_index], before_real, before_imag)
            chain_blocks.append(jnp.stack([before_real, before_imag]))
        results.append(jnp.stack(chain_blocks, axis=1))
    return jnp.stack(results, axis=1)
```

```python
import jax
import jax.numpy as jnp
from jax import lax
from jax.sharding import PartitionSpec as P

broadening = 0.6


def dot_nn(left, right):
    return lax.dot_general(left, right, (((1,), (0,)), ((), ())), preferred_element_type=jnp.float32)


def dot_nt(left, right):
    return lax.dot_general(left, right, (((1,), (1,)), ((), ())), preferred_element_type=jnp.float32)


def local(energies, hamiltonian, coupling, seed_inverse, lead_green):
    segs = lax.axis_size("seg")
    tiles = lax.axis_size("tr")
    seg = lax.axis_index("seg")
    tr = lax.axis_index("tr")
    width = lead_green.shape[3]
    order = lead_green.shape[2]
    half = 2 * width
    energy = energies[0]
    seed_re = [seed_inverse[0, 0, s] for s in range(2)]
    seed_im = [seed_inverse[1, 0, s] for s in range(2)]

    def times_seed(rows, slab):
        p = dot_nt(rows, seed_re[slab])
        q = dot_nt(rows, seed_im[slab])
        return jnp.concatenate([p[:half] - q[half:], p[half:] + q[:half]], axis=0)

    def gather_lead():
        whole = jnp.swapaxes(lead_green[:, 0], 1, 2)
        whole = jnp.where(seg == 0, whole, jnp.zeros_like(whole))
        blocks = whole.reshape(2, 1, width, order)
        for bit in (2, 8, 1, 4):
            pairs = [(t, t ^ bit) for t in range(tiles)]
            other = lax.ppermute(blocks, ("seg", "tr"), pairs)
            high = (tr & bit) != 0
            blocks = jnp.concatenate(
                [jnp.where(high, other, blocks), jnp.where(high, blocks, other)], axis=1
            )
        blocks = blocks.reshape(2, 2, 2, 2, 2, width, order)
        blocks = jnp.transpose(blocks, (0, 3, 1, 4, 2, 5, 6))
        return blocks.reshape(2, tiles * width, order)

    lead = gather_lead()

    hot = (
        lax.broadcasted_iota(jnp.int32, (width, order), 1)
        == lax.broadcasted_iota(jnp.int32, (width, order), 0) + tr * width
    ).astype(jnp.bfloat16)
    none = jnp.zeros((width, order), jnp.bfloat16)
    first = [
        jnp.concatenate([hot, none, none, none], axis=0),
        jnp.concatenate([none, hot, none, none], axis=0),
    ]

    leftward = [(s, s - 1) for s in range(1, segs)]
    rightward = [(s, s + 1) for s in range(segs - 1)]

    kept = []
    rows = first[1]
    for step in range(segs):
        inner_b = times_seed(rows, 1).astype(jnp.bfloat16)
        middle = dot_nn(inner_b, coupling[1]).astype(jnp.bfloat16)
        if step == 0:
            middle = middle + first[0]
        inner_a = times_seed(middle, 0).astype(jnp.bfloat16)
        leaving = dot_nn(inner_a, coupling[0]).astype(jnp.bfloat16)
        kept.append((inner_a, inner_b, leaving))
        if step < segs - 1:
            rows = lax.ppermute(leaving, "seg", leftward)

    def bias_of(inner, slab):
        wide = inner.astype(jnp.float32)
        turned = jnp.concatenate([-wide[half:], wide[:half]], axis=0)
        return energy * wide + broadening * turned - dot_nt(inner, hamiltonian[slab])

    def entering(leaving):
        p = dot_nn(leaving, lead[0])
        q = dot_nn(leaving, lead[1])
        return jnp.concatenate([p[:half] - q[half:], p[half:] + q[:half]], axis=0)

    def slab_step(inner, bias, came, slab):
        probe = (bias - dot_nt(came, coupling[slab])).astype(jnp.bfloat16)
        return (2.0 * inner.astype(jnp.float32) - times_seed(probe, slab)).astype(jnp.bfloat16)

    passed = jnp.zeros_like(rows)
    for step in reversed(range(segs)):
        inner_a, inner_b, leaving = kept[step]
        came = (passed.astype(jnp.float32) + entering(leaving)).astype(jnp.bfloat16)
        green_a = slab_step(inner_a, bias_of(inner_a, 0), came, 0)
        green_b = slab_step(inner_b, bias_of(inner_b, 1), green_a, 1)
        if step > 0:
            passed = lax.ppermute(green_b, "seg", rightward)

    out_a = jnp.stack([green_a[:width], green_a[half : half + width]])
    out_b = jnp.stack([green_b[width:half], green_b[half + width :]])
    out = jnp.stack([out_a, out_b], axis=1)[:, None]
    return jnp.swapaxes(out, 3, 4)


def solution(mesh):
    in_specs = (
        P(),
        P("seg", None, None),
        P("seg", None, None),
        P(None, None, "seg", None, None),
        P(None, None, None, "tr"),
    )
    out_specs = P(None, None, "seg", None, "tr")
    return jax.shard_map(local, mesh=mesh, in_specs=in_specs, out_specs=out_specs, check_vma=False)
```

```python
import functools

import jax
import jax.numpy as jnp
from jax import lax
from jax.experimental import pallas as pl
from jax.experimental.pallas import tpu as pltpu
from jax.sharding import PartitionSpec as P

broadening = 0.6
VMEM = pl.BlockSpec(memory_space=pltpu.VMEM)
SMEM = pl.BlockSpec(memory_space=pltpu.SMEM)
ANY = pl.BlockSpec(memory_space=pl.ANY)


def dot_nn(left, right):
    return lax.dot_general(left, right, (((1,), (0,)), ((), ())), preferred_element_type=jnp.float32)


def dot_nt(left, right):
    return lax.dot_general(left, right, (((1,), (1,)), ((), ())), preferred_element_type=jnp.float32)


def turned(rows):
    half = rows.shape[0] // 2
    return jnp.concatenate([-rows[half:], rows[:half]], axis=0)


def paired(rows):
    return jnp.concatenate([rows, turned(rows)], axis=1)


def call(body, out_shape, in_specs, limit_mib, name, aliases=None):
    return pl.pallas_call(
        body,
        out_shape=out_shape,
        in_specs=in_specs,
        out_specs=jax.tree.map(lambda _: VMEM, out_shape),
        compiler_params=pltpu.CompilerParams(vmem_limit_bytes=limit_mib << 20),
        input_output_aliases=aliases or {},
        name=name,
    )


def times_raw_seed(rows, seeds, slab):
    return dot_nt(rows, seeds[0, 0, slab]) + dot_nt(turned(rows), seeds[1, 0, slab])


def first_body(width, place, seeds, couple, inner, leaving):
    order = couple.shape[1]
    near = 2 * place[0]
    at_row = lax.broadcasted_iota(jnp.int32, (4 * width, order), 0)
    at_col = lax.broadcasted_iota(jnp.int32, (4 * width, order), 1)
    leaving[...] = jnp.zeros_like(leaving)

    def step(count, _):
        slab = 1 - count
        spot = at_row - slab * width
        hot = (spot >= 0) & (spot < width) & (at_col == spot + place[2] * width)
        rows = jnp.where(hot, 1.0, leaving[...].astype(jnp.float32)).astype(jnp.bfloat16)
        mid = times_raw_seed(rows, seeds, slab).astype(jnp.bfloat16)
        inner[near + slab] = mid
        leaving[...] = dot_nn(mid, couple[slab]).astype(jnp.bfloat16)
        return 0

    lax.fori_loop(0, 2, step, 0)


def second_body(place, rows, seeds, couple, inner_in, inner, leaving):
    leaving[...] = rows[...]

    @pl.when(place[0] != 0)
    def _():
        def step(count, _):
            slab = 1 - count
            mid = times_raw_seed(leaving[...], seeds, slab).astype(jnp.bfloat16)
            inner[slab] = mid
            leaving[...] = dot_nn(mid, couple[slab]).astype(jnp.bfloat16)
            return 0

        lax.fori_loop(0, 2, step, 0)


def flip_seeds_body(token, seeds, flipped):
    order = flipped.shape[2]
    for slab in range(2):
        for part in range(2):
            flipped[slab, part * order : (part + 1) * order, :] = seeds[part, 0, slab].T


def flip_links_body(token, near, far, flipped, far_flipped):
    for slab in range(2):
        flipped[slab] = near[slab].T
        far_flipped[slab] = far[slab].T


def in_chip_order(place, near, far, run):
    @pl.when(place[0] == 0)
    def _():
        run(0, *near)
        run(2, *far)

    @pl.when(place[0] != 0)
    def _():
        run(0, *far)
        run(2, *near)


def leave_body(place, rows, flipped, links, far_flipped, far_links, inner, leaving):
    leaving[...] = rows[...]

    def run(start, seeds, couple):
        def step(count, _):
            slab = 1 - count
            mid = dot_nn(paired(leaving[...]), seeds[slab]).astype(jnp.bfloat16)
            inner[start + slab] = mid
            leaving[...] = dot_nn(mid, couple[slab]).astype(jnp.bfloat16)
            return 0

        lax.fori_loop(0, 2, step, 0)

    @pl.when(place[0] == 0)
    def _():
        run(2, far_flipped, far_links)
        run(0, flipped, links)

    @pl.when(place[0] != 0)
    def _():
        run(2, flipped, links)
        run(0, far_flipped, far_links)


def bias_body(place, energy, inner, onsite, far_onsite, leaving, lead, other_lead, bias, entering):
    level = energy[0]
    near = 2 * place[0]
    for start, matrix in ((near, onsite), (2 - near, far_onsite)):

        def step(slab, _):
            rows = inner[start + slab]
            wide = rows.astype(jnp.float32)
            bias[start + slab] = level * wide + broadening * turned(wide) - dot_nn(rows, matrix[slab])
            return 0

        lax.fori_loop(0, 2, step, 0)

    @pl.when(place[1] == 0)
    def _():
        rows = leaving[...]
        around = turned(rows)
        mine = jnp.where(place[0] == 0, rows, around)
        others = jnp.where(place[0] == 0, around, rows)
        entering[...] = (dot_nn(mine, lead[...]) + dot_nn(others, other_lead[...])).astype(jnp.bfloat16)

    @pl.when(place[1] != 0)
    def _():
        entering[...] = jnp.zeros_like(entering)


def through_slab(onward, seeds, flipped_links, inner, bias, slab, place):
    probe = (bias[place] - dot_nn(onward[...], flipped_links[slab])).astype(jnp.bfloat16)
    back = dot_nn(paired(probe), seeds[slab])
    onward[...] = (2.0 * inner[place].astype(jnp.float32) - back).astype(jnp.bfloat16)


def return_body(place, passed, entering, flipped, links, far_flipped, far_links, inner, bias, onward):
    onward[...] = jnp.where(place[1] == 0, entering[...], passed[...])

    def run(start, seeds, couple):
        def step(slab, _):
            through_slab(onward, seeds, couple, inner, bias, slab, start + slab)
            return 0

        lax.fori_loop(0, 2, step, 0)

    in_chip_order(place, (flipped, links), (far_flipped, far_links), run)


def last_body(width, place, passed, entering, flipped, links, far_flipped, far_links, inner, bias, green, onward):
    onward[...] = jnp.where(place[1] == 0, entering[...], passed[...])

    @pl.when(place[0] != 0)
    def _():
        def step(slab, _):
            through_slab(onward, far_flipped, far_links, inner, bias, slab, slab)
            return 0

        lax.fori_loop(0, 2, step, 0)

    for slab in range(2):
        through_slab(onward, flipped, links, inner, bias, slab, 2 * place[0] + slab)
        for part in range(2):
            start = (2 * part + slab) * width
            green[part, 0, slab] = onward[start : start + width]


def merge_body(bit, spots, place, token, mine, other, out):
    high = (place[2] // bit) % 2
    for index, block in enumerate((mine, other)):
        for slot in range(block.shape[0]):
            out[spots(slot, high ^ index)] = block[slot]


def local(energies, hamiltonian, coupling, seed_inverse, lead_green):
    segs = lax.axis_size("seg")
    tiles = lax.axis_size("tr")
    seg = lax.axis_index("seg")
    tr = lax.axis_index("tr")
    core = seg % 2
    width = lead_green.shape[3]
    order = lead_green.shape[2]
    chips = segs // 2
    place = jnp.stack([core, seg // 2, tr])

    swap = [(s, s ^ 1) for s in range(segs)]
    leftward = [(s, (s - 2) % segs) for s in range(segs)]
    rightward = [(s, (s + 2) % segs) for s in range(segs)]

    far_seeds = lax.ppermute(seed_inverse, "seg", swap)
    far_couple = lax.ppermute(coupling, "seg", swap)
    far_onsite = lax.ppermute(hamiltonian, "seg", swap)

    def among_first(value, flip_seg, flip_tr):
        pairs = [(s * tiles + t, (s ^ flip_seg) * tiles + (t ^ flip_tr)) for s in range(2) for t in range(tiles)]
        return lax.ppermute(value, ("seg", "tr"), pairs)

    def merged(mine, other, bit, spots, token):
        shape = jax.ShapeDtypeStruct((2 * mine.shape[0],) + mine.shape[1:], jnp.bfloat16)
        body = functools.partial(merge_body, bit, spots)
        return call(body, shape, [SMEM, ANY, VMEM, VMEM], 8, "merge")(place, token, mine, other)

    rows_shape = jax.ShapeDtypeStruct((4 * width, order), jnp.bfloat16)
    inner_shape = jax.ShapeDtypeStruct((4, 4 * width, order), jnp.bfloat16)
    bias_shape = jax.ShapeDtypeStruct((4, 4 * width, order), jnp.float32)
    square = jax.ShapeDtypeStruct((2, order, order), jnp.bfloat16)
    tall = jax.ShapeDtypeStruct((2, 2 * order, order), jnp.bfloat16)
    green_shape = jax.ShapeDtypeStruct((2, 1, 2, width, order), jnp.bfloat16)

    lead = jnp.swapaxes(jnp.where(core == 0, lead_green[0, 0], lead_green[1, 0]), 0, 1)[None]
    other = among_first(lead, 0, 2)

    inner, rows = call(
        functools.partial(first_body, width), (inner_shape, rows_shape), [SMEM, VMEM, VMEM], 16, "first"
    )(place, seed_inverse, coupling)
    lead = merged(lead, other, 2, lambda slot, high: high, rows)
    other = among_first(lead, 0, 8)
    flipped = call(flip_seeds_body, tall, [ANY, VMEM], 16, "flip")(rows, seed_inverse)
    inner, rows = call(
        second_body, (inner_shape, rows_shape), [SMEM] + [VMEM] * 3 + [ANY], 16, "second", {4: 0}
    )(place, rows, far_seeds, far_couple, inner)
    lead = merged(lead, other, 8, lambda slot, high: 2 * high + slot, rows)
    other = among_first(lead, 0, 1)
    far_flipped = call(flip_seeds_body, tall, [ANY, VMEM], 16, "flip")(rows, far_seeds)
    kept = [(inner, rows)]
    for step in range(1, chips):
        rows = lax.ppermute(rows, "seg", leftward)
        inner, rows = call(leave_body, (inner_shape, rows_shape), [SMEM] + [VMEM] * 5, 20, "leave")(
            place, rows, flipped, coupling, far_flipped, far_couple
        )
        kept.append((inner, rows))
        if step == 1:
            lead = merged(lead, other, 1, lambda slot, high: 4 * high + slot, rows)
            other = among_first(lead, 0, 4)
            links, far_links = call(flip_links_body, (square, square), [ANY, VMEM, VMEM], 16, "flip_links")(
                rows, coupling, far_couple
            )
        if step == 2:
            lead = merged(
                lead,
                other,
                4,
                lambda slot, high: 8 * (slot // 2 % 2) + 4 * high + 2 * (slot % 2) + slot // 4,
                rows,
            )
            other = among_first(lead, 1, 0)
    lead, other_lead = (part.reshape(order, order) for part in (lead, other))

    passed = jnp.zeros((4 * width, order), jnp.bfloat16)
    for step in reversed(range(chips)):
        inner, leaving = kept[step]
        bias, entering = call(
            bias_body, (bias_shape, rows_shape), [SMEM, SMEM] + [VMEM] * 6, 16, "bias"
        )(place, energies, inner, hamiltonian, far_onsite, leaving, lead, other_lead)
        held = (place, passed, entering, flipped, links, far_flipped, far_links, inner, bias)
        if step > 0:
            passed = call(return_body, rows_shape, [SMEM] + [VMEM] * 8, 20, "return")(*held)
            passed = lax.ppermute(passed, "seg", rightward)
        else:
            green, _ = call(
                functools.partial(last_body, width), (green_shape, rows_shape), [SMEM] + [VMEM] * 8, 20, "last"
            )(*held)
    return jnp.swapaxes(green, 3, 4)


def solution(mesh):
    in_specs = (
        P(),
        P("seg", None, None),
        P("seg", None, None),
        P(None, None, "seg", None, None),
        P(None, None, None, "tr"),
    )
    out_specs = P(None, None, "seg", None, "tr")
    return jax.shard_map(local, mesh=mesh, in_specs=in_specs, out_specs=out_specs, check_vma=False)
```

```python
import functools

import jax
import jax.numpy as jnp
from jax import lax
from jax.experimental import pallas as pl
from jax.experimental.pallas import tpu as pltpu
from jax.sharding import PartitionSpec as P


broadening = 0.6
VMEM = pl.BlockSpec(memory_space=pltpu.VMEM)
SMEM = pl.BlockSpec(memory_space=pltpu.SMEM)
ANY = pl.BlockSpec(memory_space=pl.ANY)


def dot_nn(left, right):
    return lax.dot_general(left, right, (((1,), (0,)), ((), ())), preferred_element_type=jnp.float32)


def turned(rows):
    half = rows.shape[0] // 2
    return jnp.concatenate([-rows[half:], rows[:half]], axis=0)


def paired(rows):
    return jnp.concatenate([rows, turned(rows)], axis=1)


def call(body, out_shape, in_specs, limit_mib, grid=()):
    return pl.pallas_call(
        body,
        out_shape=out_shape,
        grid=grid,
        in_specs=in_specs,
        out_specs=jax.tree.map(lambda _: VMEM, out_shape),
        compiler_params=pltpu.CompilerParams(vmem_limit_bytes=limit_mib << 20),
    )


def in_hbm(value):
    return pltpu.with_memory_space_constraint(value, pltpu.HBM)


def one_slab(order, slab):
    return [
        pl.BlockSpec((2, 1, 1, order, order), lambda _: (0, 0, slab, 0, 0)),
        pl.BlockSpec((1, order, order), lambda _: (slab, 0, 0)),
    ]


def first_body(width, slab, place, *refs):
    rows = refs[0] if slab == 0 else None
    seeds, couple, inner, flipped, leaving = refs[-5:]
    order = couple.shape[1]
    for part in range(2):
        flipped[part * order : (part + 1) * order, :] = seeds[part, 0, 0].T
    if rows is None:
        inner[...] = jnp.zeros_like(inner)
    else:
        inner[...] = dot_nn(paired(rows[...]), flipped[...]).astype(jnp.bfloat16)
    for part in range(2):
        target = (2 * part + slab) * width
        source = pl.multiple_of(part * order + place[2] * width, width)
        inner[target : target + width, :] = flipped[pl.ds(source, width), :]
    leaving[...] = dot_nn(inner[...], couple[0]).astype(jnp.bfloat16)


def second_body(slab, place, rows, flipped, couple, *refs):
    inner, leaving = refs[-2:]

    @pl.when(place[0] == 0)
    def _():
        leaving[...] = rows[...]

    if slab == 1:

        @pl.when(place[0] == 0)
        def _():
            inner[...] = jnp.zeros_like(inner)

        @pl.when(place[0] != 0)
        def _():
            mid = dot_nn(paired(rows[...]), flipped[...]).astype(jnp.bfloat16)
            inner[...] = mid
            leaving[...] = dot_nn(mid, couple[slab]).astype(jnp.bfloat16)

    else:
        near_low, near_high, far_high = refs[:-2]

        @pl.when(place[0] == 0)
        def _():
            inner[0] = near_low[...]
            inner[1] = near_high[...]
            inner[2] = jnp.zeros_like(rows)
            inner[3] = far_high[...]

        @pl.when(place[0] != 0)
        def _():
            mid = dot_nn(paired(rows[...]), flipped[...]).astype(jnp.bfloat16)
            leaving[...] = dot_nn(mid, couple[slab]).astype(jnp.bfloat16)
            inner[0] = mid
            inner[1] = far_high[...]
            inner[2] = near_low[...]
            inner[3] = near_high[...]


def pack_body(place, token, near_low, near_high, far_low, far_high, near_links, far_links, flipped, links):
    near = 2 * place[0]
    far = 2 - near
    for spot, low, high, couple in ((near, near_low, near_high, near_links), (far, far_low, far_high, far_links)):
        flipped[spot] = low[...]
        flipped[spot + 1] = high[...]
        for slab in range(2):
            links[spot + slab] = couple[slab]


def flip_links_body(token, links, flipped_links):
    def step(slab, _):
        flipped_links[slab] = links[slab].T
        return 0

    lax.fori_loop(0, 4, step, 0)


def leave_body(rows, flipped, links, inner, leaving):
    leaving[...] = rows[...]

    def step(count, _):
        slab = 3 - count
        mid = dot_nn(paired(leaving[...]), flipped[slab]).astype(jnp.bfloat16)
        inner[slab] = mid
        leaving[...] = dot_nn(mid, links[slab]).astype(jnp.bfloat16)
        return 0

    lax.fori_loop(0, 4, step, 0)


def bias_body(place, energy, inner, onsite, far_onsite, bias):
    level = energy[0]
    near = 2 * place[0]
    for start, matrix in ((near, onsite), (2 - near, far_onsite)):

        def step(slab, _):
            rows = inner[start + slab]
            wide = rows.astype(jnp.float32)
            bias[start + slab] = level * wide + broadening * turned(wide) - dot_nn(rows, matrix[slab])
            return 0

        lax.fori_loop(0, 2, step, 0)


def enter_body(place, leaving, lead, other_lead, entering):
    @pl.when(place[1] == 0)
    def _():
        rows = leaving[...]
        around = turned(rows)
        mine = jnp.where(place[0] == 0, rows, around)
        others = jnp.where(place[0] == 0, around, rows)
        entering[...] = (dot_nn(mine, lead[...]) + dot_nn(others, other_lead[...])).astype(jnp.bfloat16)

    @pl.when(place[1] != 0)
    def _():
        entering[...] = jnp.zeros_like(entering)


def through_slab(onward, flipped, flipped_links, inner, bias, slab):
    probe = (bias[slab] - dot_nn(onward[...], flipped_links[slab])).astype(jnp.bfloat16)
    back = dot_nn(paired(probe), flipped[slab])
    onward[...] = (2.0 * inner[slab].astype(jnp.float32) - back).astype(jnp.bfloat16)


def return_body(place, passed, entering, flipped, flipped_links, inner, bias, onward):
    onward[...] = jnp.where(place[1] == 0, entering[...], passed[...])

    def step(slab, _):
        through_slab(onward, flipped, flipped_links, inner, bias, slab)
        return 0

    lax.fori_loop(0, 4, step, 0)


def last_body(width, place, passed, entering, flipped, flipped_links, inner, bias, green, onward):
    onward[...] = jnp.where(place[1] == 0, entering[...], passed[...])
    near = 2 * place[0]

    def step(slab, _):
        through_slab(onward, flipped, flipped_links, inner, bias, slab)
        for own in range(2):

            @pl.when(slab == near + own)
            def _():
                for part in range(2):
                    start = (2 * part + own) * width
                    green[part, 0, own] = onward[start : start + width]

        return 0

    lax.fori_loop(0, near + 2, step, 0)


def merge_body(bit, spots, place, token, mine, other, out):
    high = (place[2] // bit) % 2
    for index, block in enumerate((mine, other)):
        for slot in range(block.shape[0]):
            out[spots(slot, high ^ index)] = block[slot]


def pick_body(place, lead, part):
    part[0] = lead[place[0]]


def local(energies, hamiltonian, coupling, seed_inverse, lead_green):
    segs = lax.axis_size("seg")
    tiles = lax.axis_size("tr")
    seg = lax.axis_index("seg")
    tr = lax.axis_index("tr")
    core = seg % 2
    width = lead_green.shape[3]
    order = lead_green.shape[2]
    chips = segs // 2
    place = jnp.stack([core, seg // 2, tr])

    swap = [(s, s ^ 1) for s in range(segs)]
    leftward = [(s, s - 2) for s in range(2, segs)]
    rightward = [(s, (s + 2) % segs) for s in range(segs)]

    def among_first(value, flip_seg, flip_tr):
        pairs = [(s * tiles + t, (s ^ flip_seg) * tiles + (t ^ flip_tr)) for s in range(2) for t in range(tiles)]
        return lax.ppermute(value, ("seg", "tr"), pairs)

    def merged(mine, other, bit, spots, token):
        shape = jax.ShapeDtypeStruct((2 * mine.shape[0],) + mine.shape[1:], jnp.bfloat16)
        body = functools.partial(merge_body, bit, spots)
        return call(body, shape, [SMEM, ANY, VMEM, VMEM], 8)(place, token, mine, other)

    rows_shape = jax.ShapeDtypeStruct((4 * width, order), jnp.bfloat16)
    inner_shape = jax.ShapeDtypeStruct((4, 4 * width, order), jnp.bfloat16)
    bias_shape = jax.ShapeDtypeStruct((4, 4 * width, order), jnp.float32)
    square = jax.ShapeDtypeStruct((4, order, order), jnp.bfloat16)
    tall = jax.ShapeDtypeStruct((2 * order, order), jnp.bfloat16)
    talls = jax.ShapeDtypeStruct((4, 2 * order, order), jnp.bfloat16)
    green_shape = jax.ShapeDtypeStruct((2, 1, 2, width, order), jnp.bfloat16)

    far_links = lax.ppermute(coupling, "seg", swap)
    raw = (in_hbm(seed_inverse), in_hbm(coupling))
    near_high, flipped_high, rows = call(
        functools.partial(first_body, width, 1), (rows_shape, tall, rows_shape), [SMEM] + one_slab(order, 1), 20, (1,)
    )(place, *raw)
    far_flipped_high = lax.ppermute(flipped_high, "seg", swap)
    near_low, flipped_low, rows = call(
        functools.partial(first_body, width, 0),
        (rows_shape, tall, rows_shape),
        [SMEM, VMEM] + one_slab(order, 0),
        20,
        (1,),
    )(place, rows, *raw)
    far_flipped_low = lax.ppermute(flipped_low, "seg", swap)
    far_onsite = lax.ppermute(hamiltonian, "seg", swap)

    doublings = [
        (1, 1, lambda slot, high: high),
        (4, 4, lambda slot, high: 2 * high + slot),
        (3, 2, lambda slot, high: 4 * high + slot),
        (12, 8, lambda slot, high: 8 * high + 4 * (slot // 2 % 2) + 2 * (slot // 4) + slot % 2),
    ]
    part_shape = jax.ShapeDtypeStruct((1, width, order), jnp.bfloat16)
    lead = call(pick_body, part_shape, [SMEM, VMEM], 2)(place, jnp.swapaxes(lead_green[:, 0], 1, 2))
    other = among_first(lead, 0, doublings[0][0])
    lead = merged(lead, other, *doublings[0][1:], rows)
    other = among_first(lead, 0, doublings[1][0])

    far_high, rows = call(
        functools.partial(second_body, 1), (rows_shape, rows_shape), [SMEM, VMEM, VMEM, VMEM], 12
    )(place, rows, far_flipped_high, far_links)
    inner, rows = call(
        functools.partial(second_body, 0), (inner_shape, rows_shape), [SMEM] + [VMEM] * 6, 12
    )(place, rows, far_flipped_low, far_links, near_low, near_high, far_high)
    kept = [(inner, rows)]

    for step in range(1, chips):
        before = rows
        rows = lax.ppermute(rows, "seg", leftward)
        lead = merged(lead, other, *doublings[step][1:], before)
        if step < 3:
            other = among_first(lead, 0, doublings[step + 1][0])
        else:
            other = among_first(lead, 1, 0)
        if step == 1:
            flipped, links = call(pack_body, (talls, square), [SMEM, ANY] + [VMEM] * 6, 8)(
                place, before, flipped_low, flipped_high, far_flipped_low, far_flipped_high, coupling, far_links
            )
        if step == 3:
            flipped_links = call(flip_links_body, square, [ANY, VMEM], 12)(before, links)
        inner, rows = call(leave_body, (inner_shape, rows_shape), [VMEM] * 3, 12)(
            rows, flipped, links
        )
        kept.append((inner, rows))
    lead, other_lead = (part.reshape(order, order) for part in (lead, other))

    passed = jnp.zeros((4 * width, order), jnp.bfloat16)
    for step in reversed(range(chips)):
        inner, leaving = kept[step]
        bias = call(bias_body, bias_shape, [SMEM, SMEM] + [VMEM] * 3, 12)(
            place, energies, inner, hamiltonian, far_onsite
        )
        entering = call(enter_body, rows_shape, [SMEM] + [VMEM] * 3, 10)(place, leaving, lead, other_lead)
        held = (place, passed, entering, flipped, flipped_links, inner, bias)
        if step > 0:
            passed = call(return_body, rows_shape, [SMEM] + [VMEM] * 6, 12)(*held)
            passed = lax.ppermute(passed, "seg", rightward)
        else:
            green, _ = call(
                functools.partial(last_body, width), (green_shape, rows_shape), [SMEM] + [VMEM] * 6, 12
            )(*held)
    return jnp.swapaxes(green, 3, 4)


def solution(mesh):
    in_specs = (
        P(),
        P("seg", None, None),
        P("seg", None, None),
        P(None, None, "seg", None, None),
        P(None, None, None, "tr"),
    )
    out_specs = P(None, None, "seg", None, "tr")
    return jax.shard_map(local, mesh=mesh, in_specs=in_specs, out_specs=out_specs, check_vma=False)
```
